128 devices in a mesh: dp: 8 (over x, core), mp: 16 (over z, y).
Axes of the slice: x: 4, y: 4, z: 4, core: 2. Of those that a mesh axis runs over, the one named last changes fastest.
Arguments:
- canvas: bfloat16 [16, 16, 16, 1408], P('dp'), may hold values from -6 to 6
- target: bfloat16 [16, 16, 16, 1408], P('dp'), may hold values from -6 to 6
- kernel: float32 [49, 1408], replicated, may hold values from -0.875 to 0.875
- kernel_bias: float32 [1408], replicated, may hold values from -3 to 3
- norm_gain: float32 [1408], replicated, may hold values from 0.5 to 1.5
- norm_bias: float32 [1408], replicated, may hold values from -2 to 2
- in_weight: bfloat16 [5632, 1408], P('mp'), may hold values from -0.15625 to 0.15625
- in_bias: float32 [5632], P('mp'), may hold values from -3 to 3
- out_weight: bfloat16 [5632, 1408], P('mp'), may hold values from -0.078125 to 0.078125
- out_bias: float32 [1408], replicated, may hold values from -3 to 3
- probe_vector: float32 [49, 1408], P(None, 'mp'), may hold values from -6 to 6
- shapes: int32 [16, 2], P('dp'), may hold values from 2 to 16, as said below
- send_slots: int32 [16, 16, 16], P('dp'), may hold values from -1 to 447, as said below
Outputs:
- krylov_vector: float32 [49, 1408], P(None, 'mp')
- first_rayleigh: float32 [1], replicated
- lanczos_terms: float32 [3], replicated
The draws below stay inside these ranges and needn't reach their ends.
Inputs may be any that keep to these rules, and one draw needn't show every extreme that they name: `shapes`: one of an image's two sides equals 16. `send_slots`: A cell's entry is -1 exactly where it lies outside its image; otherwise it is d * 56 + k: the cell goes to slot k of the owner with dp index d. No two cells of one dp index share an entry, so none sends more than 56 cells to one owner; every owner receives exactly 256 cells over all dp indices; some dp index sends 56 cells to every owner.
All inputs are finite; a program needn't handle non-finite values.
Results may differ from the reference program's by a relative error of at most 0.025.
Values may be sent and summed in bfloat16 or wider, within the bound.
A program may use at most 128 MiB of HBM per device.

```python
import jax
import jax.numpy as jnp
from jax import lax

C = 1408
H = 5632
KS = 7
SIDE = 16
IMG_DEV = 2
TAPS = 49
IMAGES = 16
CAP = 56
TOKENS = 2048
N_MP = 16


def image_layout(key):
    source_count = IMAGES // IMG_DEV
    half_count = source_count // 2
    narrow = SIDE // 8
    broad = SIDE - narrow
    seed_key = jax.random.fold_in(key, 7)
    key_widths, key_pick, key_side, key_turn = jax.random.split(seed_key, 4)
    widths = jax.random.randint(key_widths, (half_count, IMG_DEV), narrow, broad + 1)
    chosen = jax.random.randint(key_pick, (), 0, half_count)
    upper_half = jax.random.randint(key_side, (), 0, 2)
    forced = jnp.where(upper_half == 1, narrow, broad)
    widths = jnp.where((jnp.arange(half_count) == chosen)[:, None], forced, widths)
    extents = jnp.concatenate([widths, SIDE - widths], axis=0).reshape(IMAGES)
    turned = jax.random.randint(key_turn, (IMAGES,), 0, 2)
    heights = jnp.where(turned == 1, extents, SIDE)
    breadths = jnp.where(turned == 1, SIDE, extents)
    shape_table = jnp.stack([heights, breadths], axis=1).astype(jnp.int32)
    cells_axis = jnp.arange(SIDE)
    inside = (cells_axis[None, :, None] < heights[:, None, None]) & (cells_axis[None, None, :] < breadths[:, None, None])
    inside_flat = inside.reshape(source_count, IMG_DEV * SIDE * SIDE).astype(jnp.int32)
    local_index = jnp.cumsum(inside_flat, axis=1) - inside_flat
    totals = jnp.sum(inside_flat, axis=1)
    offsets = jnp.cumsum(totals) - totals
    global_index = offsets[:, None] + local_index
    owner_index = global_index % source_count
    slot_table = jnp.where(inside_flat == 1, owner_index * CAP + local_index // source_count, -1)
    return (shape_table, slot_table.reshape(IMAGES, SIDE, SIDE).astype(jnp.int32))


def draw_shapes(key, part):
    return image_layout(key)[0]


def draw_send_slots(key, part):
    return image_layout(key)[1]


def block_levels(stream_key, dims, shards, low, high):
    def one(dim, blocks):
        steps = jax.random.uniform(jax.random.fold_in(jax.random.fold_in(stream_key, 6), dim), (blocks,), jnp.float32, low / len(shards), high / len(shards))
        return jnp.repeat(jnp.exp(steps), dims[dim] // blocks).reshape((-1,) + (1,) * (len(dims) - dim - 1))

    loudness = one(*shards[0])
    for cut in shards[1:]:
        loudness = loudness * one(*cut)
    return loudness


def normal_values(stream_key, extent, spread, limit, cuts=(), held_as=jnp.bfloat16):
    drawn = spread * jax.random.normal(stream_key, extent, jnp.float32)
    if cuts:
        drawn = drawn * block_levels(stream_key, extent, cuts, -0.22, 0.18)
    return jnp.clip(drawn, -limit, limit).astype(held_as)


def setup_inputs(seed: int = 0) -> dict:
    keys = jax.random.split(jax.random.key(seed), 14)
    canvas = normal_values(keys[0], (IMAGES, SIDE, SIDE, C), 1.0, 6.0, ((0, 8),))
    target = normal_values(keys[1], (IMAGES, SIDE, SIDE, C), 1.0, 6.0, ((0, 8),))
    kernel = normal_values(keys[2], (TAPS, C), TAPS ** -0.5, 0.875, (), jnp.float32)
    kernel_bias = normal_values(keys[3], (C,), 0.5, 3.0, (), jnp.float32)
    norm_gain = jnp.clip(1.0 + 0.1 * jax.random.normal(keys[4], (C,), jnp.float32), 0.5, 1.5)
    norm_bias = normal_values(keys[5], (C,), 0.3, 2.0, (), jnp.float32)
    in_weight = normal_values(keys[6], (H, C), C ** -0.5, 0.15625, ((0, 16),))
    in_bias = normal_values(keys[7], (H,), 0.5, 3.0, ((0, 16),), jnp.float32)
    out_weight = normal_values(keys[8], (H, C), H ** -0.5, 0.078125, ((0, 16),))
    out_bias = normal_values(keys[9], (C,), 0.5, 3.0, (), jnp.float32)
    probe_vector = normal_values(keys[10], (TAPS, C), 1.0, 6.0, ((1, 16),), jnp.float32)
    shapes = draw_shapes(jax.random.fold_in(keys[13], 71), 0)
    send_slots = draw_send_slots(jax.random.fold_in(keys[13], 71), 0)
    return {"canvas": canvas, "target": target, "kernel": kernel, "kernel_bias": kernel_bias, "norm_gain": norm_gain, "norm_bias": norm_bias, "in_weight": in_weight, "in_bias": in_bias, "out_weight": out_weight, "out_bias": out_bias, "probe_vector": probe_vector, "shapes": shapes, "send_slots": send_slots}


layer_eps = 1e-06
vector_eps = 1e-06
half_root = 0.7071067811865476
density_scale = 0.3989422804014327

def phi_density(values):
    return density_scale * jnp.exp(-0.5 * values * values)

def gelu_value(values):
    return 0.5 * values * (1.0 + jax.scipy.special.erf(values * half_root))

def gelu_slope(values):
    return 0.5 * (1.0 + jax.scipy.special.erf(values * half_root)) + values * phi_density(values)

def gelu_bend(values):
    return phi_density(values) * (2.0 - values * values)

def inside_mask(shapes):
    cell_axis = jnp.arange(SIDE, dtype=jnp.int32)
    tall = cell_axis[None, :, None] < shapes[:, 0][:, None, None]
    wide = cell_axis[None, None, :] < shapes[:, 1][:, None, None]
    return (tall & wide).astype(jnp.float32)

def depthwise(canvas_values, tap_weights):
    margin_cells = KS // 2
    padded = jnp.pad(canvas_values, ((0, 0), (margin_cells, margin_cells), (margin_cells, margin_cells), (0, 0)))
    running = jnp.zeros(canvas_values.shape, jnp.float32)
    for tap_row in range(KS):
        for tap_col in range(KS):
            running = running + padded[:, tap_row:tap_row + SIDE, tap_col:tap_col + SIDE, :] * tap_weights[tap_row * KS + tap_col]
    return running

def correlate(masked, grads):
    margin_cells = KS // 2
    padded = jnp.pad(masked, ((0, 0), (margin_cells, margin_cells), (margin_cells, margin_cells), (0, 0)))
    grads_wide = grads.astype(jnp.float32)
    pieces = []
    for tap_row in range(KS):
        for tap_col in range(KS):
            window = padded[:, tap_row:tap_row + SIDE, tap_col:tap_col + SIDE, :].astype(jnp.float32)
            pieces.append(jnp.einsum('npqc,npqc->c', window, grads_wide))
    return jnp.stack(pieces, 0)

def normalize(rows):
    values = rows.astype(jnp.float32)
    row_mean = lax.optimization_barrier(jnp.mean(values, 1, keepdims=True))
    centered = values - row_mean
    deviation = jnp.sqrt(lax.optimization_barrier(jnp.mean(centered * centered, 1, keepdims=True)) + layer_eps)
    return (centered / deviation, deviation)

def group_sum(first_mat, second_mat, groups):
    group_width = first_mat.shape[1] // groups
    running = jnp.zeros((first_mat.shape[0], second_mat.shape[1]), jnp.float32)
    for group in range(groups):
        partial_value = jnp.dot(first_mat[:, group * group_width:(group + 1) * group_width], second_mat[group * group_width:(group + 1) * group_width], preferred_element_type=jnp.float32)
        rounded = lax.optimization_barrier(partial_value.astype(jnp.bfloat16))
        running = running + rounded.astype(jnp.float32)
    return running

def reference(canvas, target, kernel, kernel_bias, norm_gain, norm_bias, in_weight, in_bias, out_weight, out_bias, probe_vector, shapes, send_slots):
    inside = inside_mask(shapes)
    masked = canvas * inside[..., None].astype(jnp.bfloat16)
    masked_wide = masked.astype(jnp.float32)
    conved = (depthwise(masked_wide, kernel) + kernel_bias).astype(jnp.bfloat16)
    diff = (target.astype(jnp.float32) - canvas.astype(jnp.float32)).astype(jnp.bfloat16)
    picked = jnp.nonzero(send_slots.reshape(-1) >= 0, size=TOKENS)[0].astype(jnp.int32)
    conv_rows = conved.reshape(-1, C)[picked]
    diff_rows = diff.reshape(-1, C)[picked]
    normed, deviation = normalize(conv_rows)
    features = (normed * norm_gain + norm_bias).astype(jnp.bfloat16)
    pre_act = jnp.dot(features, in_weight.T, preferred_element_type=jnp.float32) + in_bias
    activation = gelu_value(pre_act).astype(jnp.bfloat16)
    outputs = group_sum(activation, out_weight, N_MP) + out_bias
    residue = (outputs - diff_rows.astype(jnp.float32)).astype(jnp.bfloat16)
    back_act = jnp.dot(residue, out_weight.T, preferred_element_type=jnp.float32)
    slope = gelu_slope(pre_act)
    curvature = back_act * gelu_bend(pre_act)
    back_pre = (back_act * slope).astype(jnp.bfloat16)
    back_feat = group_sum(back_pre, in_weight, N_MP)
    grad_scaled = back_feat * norm_gain
    grad_mean = lax.optimization_barrier(jnp.mean(grad_scaled, 1, keepdims=True))
    grad_corr = lax.optimization_barrier(jnp.mean(grad_scaled * normed, 1, keepdims=True))
    back_conv = (grad_scaled - grad_mean - normed * grad_corr) / deviation

    def hessian(direction):
        tangent = depthwise(masked_wide, direction).astype(jnp.bfloat16).reshape(-1, C)[picked]
        tangent_vals = tangent.astype(jnp.float32)
        lift = lax.optimization_barrier(jnp.mean(normed * tangent_vals, 1, keepdims=True))
        tan_hat = (tangent_vals - lax.optimization_barrier(jnp.mean(tangent_vals, 1, keepdims=True)) - normed * lift) / deviation
        rate = lift / deviation
        tan_feat = (tan_hat * norm_gain).astype(jnp.bfloat16)
        tan_pre = jnp.dot(tan_feat, in_weight.T, preferred_element_type=jnp.float32)
        tan_act = (slope * tan_pre).astype(jnp.bfloat16)
        tan_out = group_sum(tan_act, out_weight, N_MP).astype(jnp.bfloat16)
        tan_back_pre = (jnp.dot(tan_out, out_weight.T, preferred_element_type=jnp.float32) * slope + curvature * tan_pre).astype(jnp.bfloat16)
        tan_scaled = group_sum(tan_back_pre, in_weight, N_MP) * norm_gain
        tan_mean = lax.optimization_barrier(jnp.mean(tan_scaled, 1, keepdims=True))
        tan_corr = lax.optimization_barrier(jnp.mean(tan_scaled * normed + grad_scaled * tan_hat, 1, keepdims=True))
        tan_back = ((tan_scaled - tan_mean - tan_hat * grad_corr - normed * tan_corr) / deviation - back_conv * rate).astype(jnp.bfloat16)
        grads = jnp.zeros((IMAGES * SIDE * SIDE, C), jnp.bfloat16).at[picked].set(tan_back)
        return correlate(masked, grads.reshape(IMAGES, SIDE, SIDE, C)) * (1.0 / TOKENS)
    lanczos_one = probe_vector / jnp.sqrt(jnp.sum(probe_vector * probe_vector) + vector_eps)
    product_one = hessian(lanczos_one)
    alpha_one = jnp.sum(product_one * lanczos_one)
    remainder_one = product_one - alpha_one * lanczos_one
    beta_one = jnp.sqrt(jnp.sum(remainder_one * remainder_one) + vector_eps)
    lanczos_two = remainder_one / beta_one
    product_two = hessian(lanczos_two)
    alpha_two = jnp.sum(product_two * lanczos_two)
    remainder_two = product_two - alpha_two * lanczos_two - beta_one * lanczos_one
    beta_two = jnp.sqrt(jnp.sum(remainder_two * remainder_two) + vector_eps)
    return (remainder_two / beta_two, jnp.stack([alpha_one]), jnp.stack([alpha_two, beta_one, beta_two]))
```

```python
import jax
import jax.numpy as jnp
from jax import lax
from jax.experimental import pallas as pl
from jax.experimental.pallas import tpu as pltpu
from jax.sharding import PartitionSpec as P

C = 1408
H = 5632
KS = 7
SIDE = 16
TAPS = 49
TOKENS = 2048
N_MP = 16
N_DP = 8
HPART = H // N_MP
HALF = HPART // 2
QUARTER = HALF // 2
CPART = C // N_MP
ROWS = 32
LANE = 128
CBLK = C // LANE
HBLK = 512
NHB = H // HBLK
TAPROWS = 56
TILES = 80
CHUNK = TILES // N_MP

layer_eps = 1e-06
vector_eps = 1e-06
half_root = 0.7071067811865476
density_scale = 0.3989422804014327

MESH = pl.DeviceIdType.MESH
VMEM_BIG = 64 * 1024 * 1024 - 512 * 1024
F32 = jnp.float32
BF16 = jnp.bfloat16


def vmem():
    return pl.BlockSpec(memory_space=pltpu.VMEM)


def hbm():
    return pl.BlockSpec(memory_space=pl.ANY)


def gather_kernel(
    w1_ref, w2_ref, misc_ref, o1_ref, o2_ref, om_ref, send, recv, fsend, frecv, msend, mrecv, lsem
):
    dp = lax.axis_index("dp")
    mp = lax.axis_index("mp")
    core = lax.rem(dp, 2)
    sib = dp + 1 - 2 * core
    z = mp // 4
    y = lax.rem(mp, 4)

    def at(dz, dy):
        return lax.rem(z + dz, 4) * 4 + lax.rem(y + dy, 4)

    barrier = pltpu.get_barrier_semaphore()
    for r in range(1, N_MP):
        pl.semaphore_signal(
            barrier, inc=1, device_id={"mp": lax.rem(mp + r, N_MP)}, device_id_type=MESH
        )
    pl.semaphore_signal(barrier, inc=1, device_id={"dp": sib}, device_id_type=MESH)
    pl.semaphore_wait(barrier, N_MP)

    base = pl.multiple_of(core * HALF, 8)
    own = (w1_ref, w2_ref)
    out = (o1_ref, o2_ref)
    pending = []

    def remote(src, dst, ssem, rsem, **dev):
        copy = pltpu.make_async_remote_copy(
            src_ref=src, dst_ref=dst, send_sem=ssem, recv_sem=rsem, device_id=dev, device_id_type=MESH
        )
        return copy

    def step(colour, first, second):
        return (second, first) if colour == 0 else (first, second)

    def peer(colour, axis, sign):
        d = 1 if sign == 0 else 3
        a, b = (d, 0) if axis == 0 else (0, d)
        return at(*step(colour, a, b))

    def block(colour, a, b):
        return at(*step(colour, b, a))

    def rows(part):
        if part == 2:
            return pl.ds(base, HALF)
        return pl.ds(pl.multiple_of(base + part * QUARTER, 8), QUARTER)

    slot = {}

    def transfer(colour, key, a, b, part, axis, sign):
        k = slot.setdefault(key, len(slot))
        if (a, b) == (0, 0):
            src = own[colour].at[rows(part)]
        else:
            src = out[colour].at[block(colour, a, b), rows(part)]
        dst = out[colour].at[block(colour, a, b), rows(part)]
        return remote(
            src, dst, send.at[colour, k], recv.at[colour, k], mp=peer(colour, axis, sign)
        )

    started = []

    def go(colour, key, a, b, part, axis, sign):
        copy = transfer(colour, key, a, b, part, axis, sign)
        copy.start()
        started.append(copy)
        pending.append((colour, key))
        return copy

    nforward = [0]
    forwards = []

    def forward(colour, a, b):
        k = nforward[0]
        nforward[0] += 1
        ref = out[colour].at[block(colour, a, b), rows(2)]
        copy = remote(ref, ref, fsend.at[k], frecv.at[k], dp=sib)
        copy.start()
        forwards.append(copy)

    copies = {}
    for colour in range(2):
        for sign in range(2):
            copies[colour, 0, "n", sign] = go(colour, ("n", sign), 0, 0, 2, 0, sign)
    for r in range(1, N_MP):
        copy = remote(
            misc_ref,
            om_ref.at[mp],
            msend.at[r],
            mrecv.at[r],
            mp=lax.rem(mp + r, N_MP),
        )
        copy.start()
        copies["misc", r] = copy
    local = []
    for colour in range(2):
        copy = pltpu.make_async_copy(own[colour], out[colour].at[mp], lsem.at[colour])
        copy.start()
        local.append(copy)
    copy = pltpu.make_async_copy(misc_ref, om_ref.at[mp], lsem.at[2])
    copy.start()
    local.append(copy)

    def spread(colour, b):
        for sign in range(2):
            copies[colour, 1, b, sign] = go(colour, ("z", b, sign), 0, b, 2, 1, sign)

    for colour in range(2):
        spread(colour, 0)
    for sign in range(2):
        for colour in range(2):
            copies[colour, 0, "n", sign].wait_recv()
            b = 3 if sign == 0 else 1
            copies[colour, 0, "r", sign] = go(colour, ("r", sign), 0, b, sign, 0, sign)
            spread(colour, b)
            forward(colour, 0, b)
    for colour in range(2):
        copies[colour, 0, "r", 0].wait_recv()
        copies[colour, 0, "r", 1].wait_recv()
        spread(colour, 2)
        forward(colour, 0, 2)
    for b in (0, 3, 1, 2):
        for sign in range(2):
            for colour in range(2):
                copies[colour, 1, b, sign].wait_recv()
                a = 3 if sign == 0 else 1
                copies[colour, 1, b, "r", sign] = go(
                    colour, ("zr", b, sign), a, b, sign, 1, sign
                )
                forward(colour, a, b)
    for b in (0, 3, 1, 2):
        for colour in range(2):
            copies[colour, 1, b, "r", 0].wait_recv()
            copies[colour, 1, b, "r", 1].wait_recv()
            forward(colour, 2, b)
    for r in range(1, N_MP):
        copies["misc", r].wait_recv()
        copies["misc", r].wait_send()
    for copy in forwards:
        copy.wait_recv()
    for copy in started + forwards:
        copy.wait_send()
    for copy in local:
        copy.wait()


def gather(w1, w2, misc):
    return pl.pallas_call(
        gather_kernel,
        out_shape=(
            jax.ShapeDtypeStruct((N_MP, HPART, C), BF16),
            jax.ShapeDtypeStruct((N_MP, HPART, C), BF16),
            jax.ShapeDtypeStruct((N_MP, 64, LANE), F32),
        ),
        in_specs=[vmem(), vmem(), vmem()],
        out_specs=(hbm(), hbm(), hbm()),
        scratch_shapes=[
            pltpu.SemaphoreType.DMA((2, 20)),
            pltpu.SemaphoreType.DMA((2, 20)),
            pltpu.SemaphoreType.DMA((30,)),
            pltpu.SemaphoreType.DMA((30,)),
            pltpu.SemaphoreType.DMA((N_MP,)),
            pltpu.SemaphoreType.DMA((N_MP,)),
            pltpu.SemaphoreType.DMA((3,)),
        ],
        compiler_params=pltpu.CompilerParams(collective_id=0, has_side_effects=True),
        name="gather_weights",
    )(w1, w2, misc)


def reduce_kernel(p_ref, o_ref, in1, in2, s1, r1, s2, r2, s3, r3):
    dp = lax.axis_index("dp")
    mp = lax.axis_index("mp")
    barrier = pltpu.get_barrier_semaphore()
    for r in range(1, N_MP):
        pl.semaphore_signal(
            barrier, inc=1, device_id={"mp": lax.rem(mp + r, N_MP)}, device_id_type=MESH
        )
    for r in range(1, N_DP):
        pl.semaphore_signal(
            barrier, inc=1, device_id={"dp": lax.rem(dp + r, N_DP)}, device_id_type=MESH
        )
    pl.semaphore_wait(barrier, N_MP + N_DP - 2)

    def send(src, dst, ssem, rsem, **dev):
        copy = pltpu.make_async_remote_copy(
            src_ref=src, dst_ref=dst, send_sem=ssem, recv_sem=rsem, device_id=dev, device_id_type=MESH
        )
        copy.start()
        return copy

    first = []
    for r in range(1, N_MP):
        peer = lax.rem(mp + r, N_MP)
        first.append(
            send(p_ref.at[pl.ds(peer * CHUNK, CHUNK)], in1.at[r], s1.at[r], r1.at[r], mp=peer)
        )
    total = p_ref[pl.ds(mp * CHUNK, CHUNK)]
    for r in range(1, N_MP):
        first[r - 1].wait_recv()
        total = total + in1[r]
    in2[dp] = total
    second = []
    for r in range(1, N_DP):
        peer = lax.rem(dp + r, N_DP)
        second.append(send(in2.at[dp], in2.at[dp], s2.at[r], r2.at[r], dp=peer))
    for copy in second:
        copy.wait_recv()
    total = in2[0]
    for d in range(1, N_DP):
        total = total + in2[d]
    mine = pl.ds(mp * CHUNK, CHUNK)
    o_ref[mine] = total
    third = []
    for r in range(1, N_MP):
        peer = lax.rem(mp + r, N_MP)
        third.append(send(o_ref.at[mine], o_ref.at[mine], s3.at[r], r3.at[r], mp=peer))
    for copy in third:
        copy.wait_recv()
    for copy in first + second + third:
        copy.wait_send()


def all_reduce(part, which):
    return pl.pallas_call(
        reduce_kernel,
        out_shape=jax.ShapeDtypeStruct((TILES, 8, LANE), F32),
        in_specs=[vmem()],
        out_specs=vmem(),
        scratch_shapes=[
            pltpu.VMEM((N_MP, CHUNK, 8, LANE), F32),
            pltpu.VMEM((N_DP, CHUNK, 8, LANE), F32),
            pltpu.SemaphoreType.DMA((N_MP,)),
            pltpu.SemaphoreType.DMA((N_MP,)),
            pltpu.SemaphoreType.DMA((N_DP,)),
            pltpu.SemaphoreType.DMA((N_DP,)),
            pltpu.SemaphoreType.DMA((N_MP,)),
            pltpu.SemaphoreType.DMA((N_MP,)),
        ],
        compiler_params=pltpu.CompilerParams(collective_id=1 + which, has_side_effects=True),
        name="reduce_product",
    )(part)


def rows_dot_t(left, right):
    return lax.dot_general(
        left, right, (((1,), (1,)), ((), ())), preferred_element_type=F32
    )


def rows_dot(left, right):
    return jnp.dot(left, right, preferred_element_type=F32)


def convolve(xf_ref, taps_ref, out_ref, bias_ref=None):
    def body(cb, carry):
        lanes = pl.ds(pl.multiple_of(cb * LANE, LANE), LANE)
        sums = [jnp.zeros((SIDE, LANE), F32) for _ in range(2)]
        for j in range(KS):
            for r in range(KS + 1):
                x = xf_ref[r, pl.ds(j, SIDE), lanes]
                for p in range(2):
                    i = r - p
                    if 0 <= i < KS:
                        sums[p] = sums[p] + x * taps_ref[pl.ds(i * KS + j, 1), lanes]
        for p in range(2):
            value = sums[p]
            if bias_ref is not None:
                value = value + bias_ref[:, lanes]
            out_ref[pl.ds(p * SIDE, SIDE), lanes] = value
        return carry

    lax.fori_loop(0, CBLK, body, 0)


def correlate(xf_ref, grads_ref, out_ref):
    out_ref[...] = jnp.zeros_like(out_ref)

    def body(cb, carry):
        lanes = pl.ds(pl.multiple_of(cb * LANE, LANE), LANE)
        g = [[grads_ref[pl.ds(p * SIDE + 8 * h, 8), lanes] for h in range(2)] for p in range(2)]
        for j in range(KS):
            xs = [
                [xf_ref[r, pl.ds(j + 8 * h, 8), lanes] for h in range(2)] for r in range(KS + 1)
            ]
            for i in range(KS):
                acc = xs[i][0] * g[0][0] + xs[i][1] * g[0][1]
                acc = acc + xs[i + 1][0] * g[1][0] + xs[i + 1][1] * g[1][1]
                tap = i * KS + j
                out_ref[(tap // 8) * CBLK + cb, pl.ds(tap % 8, 1), :] = jnp.sum(
                    acc, axis=0, keepdims=True
                ) * (1.0 / TOKENS)
        return carry

    lax.fori_loop(0, CBLK, body, 0)


def weight_copies(w_hbm, w_vmem, sem):
    return [
        pltpu.make_async_copy(
            w_hbm.at[pl.ds(b * HBLK, HBLK)], w_vmem.at[pl.ds(b * HBLK, HBLK)], sem.at[b]
        )
        for b in range(NHB)
    ]


def wait_block(w_hbm, w_vmem, sem, b):
    part = pl.ds(pl.multiple_of(b * HBLK, HBLK), HBLK)
    pltpu.make_async_copy(w_hbm.at[part], w_vmem.at[part], sem.at[b]).wait()


def hidden(b):
    return pl.ds(pl.multiple_of(b * HBLK, HBLK), HBLK)


def mean_rows(values):
    return jnp.sum(values, axis=1, keepdims=True) * (1.0 / C)


def hessian_rows(
    tan_ref,
    first_pass_ready,
    w1s,
    w2s,
    slope_ref,
    curv_ref,
    tpre_ref,
    acc_ref,
    grads_ref,
    normed,
    dev,
    gain,
    grad_scaled,
    grad_corr,
    back_conv,
    mask,
):
    t = tan_ref[...].astype(BF16).astype(F32)
    lift = mean_rows(normed * t)
    tan_hat = (t - mean_rows(t) - normed * lift) / dev
    rate = lift / dev
    feat = (tan_hat * gain).astype(BF16)
    acc_ref[...] = jnp.zeros_like(acc_ref)

    def forward(b, carry):
        first_pass_ready(b)
        hid = hidden(b)
        tan_pre = rows_dot_t(feat, w1s[hid, :])
        tpre_ref[:, hid] = tan_pre
        act = (slope_ref[:, hid] * tan_pre).astype(BF16)
        acc_ref[...] += rows_dot(act, w2s[hid, :])
        return carry

    lax.fori_loop(0, NHB, forward, 0)
    tan_out = acc_ref[...].astype(BF16)
    acc_ref[...] = jnp.zeros_like(acc_ref)

    def backward(b, carry):
        hid = hidden(b)
        back = rows_dot_t(tan_out, w2s[hid, :])
        back_pre = (back * slope_ref[:, hid] + curv_ref[:, hid] * tpre_ref[:, hid]).astype(BF16)
        acc_ref[...] += rows_dot(back_pre, w1s[hid, :])
        return carry

    lax.fori_loop(0, NHB, backward, 0)
    scaled = acc_ref[...] * gain
    h1 = mean_rows(scaled)
    h2 = mean_rows(scaled * normed + grad_scaled * tan_hat)
    back = (scaled - h1 - tan_hat * grad_corr - normed * h2) / dev - back_conv * rate
    grads_ref[...] = back.astype(BF16).astype(F32) * mask


def first_kernel(
    x_ref,
    diff_ref,
    mask_ref,
    kernel_ref,
    kbias_ref,
    gain_ref,
    nbias_ref,
    ibias_ref,
    obias_ref,
    probe_ref,
    w1_hbm,
    w2_hbm,
    part_ref,
    q_ref,
    slope_ref,
    curv_ref,
    normed_ref,
    dev_ref,
    gs_ref,
    gc_ref,
    bc_ref,
    w1s,
    w2s,
    xf_ref,
    tan_ref,
    acc_ref,
    tpre_ref,
    sem1,
    sem2,
):
    c1 = weight_copies(w1_hbm, w1s, sem1)
    c2 = weight_copies(w2_hbm, w2s, sem2)
    for b in range(NHB):
        c1[b].start()
        c2[b].start()
    xf_ref[...] = x_ref[...].astype(F32)
    probe = probe_ref[...]
    norm = jnp.sqrt(
        jnp.sum(jnp.sum(probe * probe, axis=1, keepdims=True), axis=0, keepdims=True) + vector_eps
    )
    q_ref[...] = probe / norm
    convolve(xf_ref, kernel_ref, tan_ref, kbias_ref)
    values = tan_ref[...].astype(BF16).astype(F32)
    centered = values - mean_rows(values)
    dev = jnp.sqrt(mean_rows(centered * centered) + layer_eps)
    normed = centered / dev
    gain = gain_ref[...]
    feat = (normed * gain + nbias_ref[...]).astype(BF16)
    convolve(xf_ref, q_ref, tan_ref)
    normed_ref[...] = normed
    dev_ref[...] = jnp.broadcast_to(dev, (ROWS, LANE))
    acc_ref[...] = jnp.zeros_like(acc_ref)

    def forward(b, carry):
        hid = hidden(b)
        wait_block(w1_hbm, w1s, sem1, b)
        pre = rows_dot_t(feat, w1s[hid, :]) + ibias_ref[:, hid]
        phi = 0.5 * (1.0 + lax.erf(pre * half_root))
        density = density_scale * jnp.exp(-0.5 * pre * pre)
        slope_ref[:, hid] = phi + pre * density
        curv_ref[:, hid] = density * (2.0 - pre * pre)
        act = (pre * phi).astype(BF16)
        wait_block(w2_hbm, w2s, sem2, b)
        acc_ref[...] += rows_dot(act, w2s[hid, :])
        return carry

    lax.fori_loop(0, NHB, forward, 0)
    residue = (acc_ref[...] + obias_ref[...] - diff_ref[...].astype(F32)).astype(BF16)
    acc_ref[...] = jnp.zeros_like(acc_ref)

    def backward(b, carry):
        hid = hidden(b)
        back = rows_dot_t(residue, w2s[hid, :])
        curv_ref[:, hid] = back * curv_ref[:, hid]
        back_pre = (back * slope_ref[:, hid]).astype(BF16)
        acc_ref[...] += rows_dot(back_pre, w1s[hid, :])
        return carry

    lax.fori_loop(0, NHB, backward, 0)
    grad_scaled = acc_ref[...] * gain
    grad_mean = mean_rows(grad_scaled)
    grad_corr = mean_rows(grad_scaled * normed)
    back_conv = (grad_scaled - grad_mean - normed * grad_corr) / dev
    gs_ref[...] = grad_scaled
    gc_ref[...] = jnp.broadcast_to(grad_corr, (ROWS, LANE))
    bc_ref[...] = back_conv
    hessian_rows(
        tan_ref,
        lambda b: None,
        w1s,
        w2s,
        slope_ref,
        curv_ref,
        tpre_ref,
        acc_ref,
        tan_ref,
        normed,
        dev,
        gain,
        grad_scaled,
        grad_corr,
        back_conv,
        mask_ref[:, 0:1],
    )
    correlate(xf_ref, tan_ref, part_ref)


def first_stage(x, diff, mask, kernel, kbias, gain, nbias, ibias, obias, probe, w1, w2):
    rows_c = jax.ShapeDtypeStruct((ROWS, C), F32)
    rows_h = jax.ShapeDtypeStruct((ROWS, H), F32)
    rows_l = jax.ShapeDtypeStruct((ROWS, LANE), F32)
    return pl.pallas_call(
        first_kernel,
        out_shape=(
            jax.ShapeDtypeStruct((TILES, 8, LANE), F32),
            jax.ShapeDtypeStruct((TAPROWS, C), F32),
            rows_h,
            rows_h,
            rows_c,
            rows_l,
            rows_c,
            rows_l,
            rows_c,
        ),
        in_specs=[vmem()] * 10 + [hbm(), hbm()],
        out_specs=tuple([vmem()] * 9),
        scratch_shapes=[
            pltpu.VMEM((H, C), BF16),
            pltpu.VMEM((H, C), BF16),
            pltpu.VMEM((KS + 1, 24, C), F32),
            pltpu.VMEM((ROWS, C), F32),
            pltpu.VMEM((ROWS, C), F32),
            pltpu.VMEM((ROWS, H), F32),
            pltpu.SemaphoreType.DMA((NHB,)),
            pltpu.SemaphoreType.DMA((NHB,)),
        ],
        compiler_params=pltpu.CompilerParams(vmem_limit_bytes=VMEM_BIG),
        name="first_stage",
    )(x, diff, mask, kernel, kbias, gain, nbias, ibias, obias, probe, w1, w2)


def total(values):
    return jnp.sum(jnp.sum(values, axis=1, keepdims=True), axis=0, keepdims=True)


def untile(w_ref, flat_ref):
    for rb in range(TAPROWS // 8):
        for cb in range(CBLK):
            flat_ref[pl.ds(8 * rb, 8), pl.ds(LANE * cb, LANE)] = w_ref[rb * CBLK + cb]


def second_kernel(
    w_ref,
    x_ref,
    mask_ref,
    gain_ref,
    q_ref,
    slope_ref,
    curv_ref,
    normed_ref,
    dev_ref,
    gs_ref,
    gc_ref,
    bc_ref,
    w1_hbm,
    w2_hbm,
    part_ref,
    q2_ref,
    terms_ref,
    w1s,
    w2s,
    xf_ref,
    tan_ref,
    acc_ref,
    tpre_ref,
    sem1,
    sem2,
):
    c1 = weight_copies(w1_hbm, w1s, sem1)
    c2 = weight_copies(w2_hbm, w2s, sem2)
    for b in range(NHB):
        c1[b].start()
        c2[b].start()
    xf_ref[...] = x_ref[...].astype(F32)
    untile(w_ref, q2_ref)
    product = q2_ref[...]
    q = q_ref[...]
    alpha = total(product * q)
    remainder = product - alpha * q
    beta = jnp.sqrt(total(remainder * remainder) + vector_eps)
    q2_ref[...] = remainder / beta
    terms_ref[pl.ds(0, 8), :] = jnp.broadcast_to(alpha, (8, LANE))
    terms_ref[pl.ds(8, 8), :] = jnp.broadcast_to(beta, (8, LANE))
    convolve(xf_ref, q2_ref, tan_ref)

    def ready(b):
        wait_block(w1_hbm, w1s, sem1, b)
        wait_block(w2_hbm, w2s, sem2, b)

    hessian_rows(
        tan_ref,
        ready,
        w1s,
        w2s,
        slope_ref,
        curv_ref,
        tpre_ref,
        acc_ref,
        tan_ref,
        normed_ref[...],
        dev_ref[:, 0:1],
        gain_ref[...],
        gs_ref[...],
        gc_ref[:, 0:1],
        bc_ref[...],
        mask_ref[:, 0:1],
    )
    correlate(xf_ref, tan_ref, part_ref)


def second_stage(w, x, mask, gain, q, saved, w1, w2):
    return pl.pallas_call(
        second_kernel,
        out_shape=(
            jax.ShapeDtypeStruct((TILES, 8, LANE), F32),
            jax.ShapeDtypeStruct((TAPROWS, C), F32),
            jax.ShapeDtypeStruct((16, LANE), F32),
        ),
        in_specs=[vmem()] * 12 + [hbm(), hbm()],
        out_specs=(vmem(), vmem(), vmem()),
        scratch_shapes=[
            pltpu.VMEM((H, C), BF16),
            pltpu.VMEM((H, C), BF16),
            pltpu.VMEM((KS + 1, 24, C), F32),
            pltpu.VMEM((ROWS, C), F32),
            pltpu.VMEM((ROWS, C), F32),
            pltpu.VMEM((ROWS, H), F32),
            pltpu.SemaphoreType.DMA((NHB,)),
            pltpu.SemaphoreType.DMA((NHB,)),
        ],
        compiler_params=pltpu.CompilerParams(vmem_limit_bytes=VMEM_BIG),
        name="second_stage",
    )(w, x, mask, gain, q, *saved, w1, w2)


def last_kernel(w_ref, q1_ref, q2_ref, terms_ref, out_ref, scal_ref):
    untile(w_ref, out_ref)
    product = out_ref[...]
    q2 = q2_ref[...]
    alpha = total(product * q2)
    beta_one = terms_ref[pl.ds(8, 1), 0:1]
    remainder = product - alpha * q2 - beta_one * q1_ref[...]
    beta = jnp.sqrt(total(remainder * remainder) + vector_eps)
    out_ref[...] = remainder / beta
    lane = lax.broadcasted_iota(jnp.int32, (8, LANE), 1)
    alpha_one = terms_ref[pl.ds(0, 1), 0:1]
    scal_ref[...] = jnp.where(
        lane == 0,
        alpha,
        jnp.where(lane == 1, beta_one, jnp.where(lane == 2, beta, alpha_one)),
    )


def last_stage(w, q1, q2, terms):
    return pl.pallas_call(
        last_kernel,
        out_shape=(
            jax.ShapeDtypeStruct((TAPROWS, C), F32),
            jax.ShapeDtypeStruct((8, LANE), F32),
        ),
        in_specs=[vmem()] * 4,
        out_specs=(vmem(), vmem()),
        name="last_stage",
    )(w, q1, q2, terms)


def per_device(
    canvas,
    target,
    kernel,
    kernel_bias,
    norm_gain,
    norm_bias,
    in_weight,
    in_bias,
    out_weight,
    out_bias,
    probe_vector,
    shapes,
    send_slots,
):
    mp = lax.axis_index("mp")
    misc = jnp.concatenate(
        [
            jnp.pad(probe_vector, ((0, TAPROWS - TAPS), (0, LANE - CPART))),
            jnp.pad(in_bias, (0, 8 * LANE - HPART)).reshape(8, LANE),
        ],
        0,
    )
    w1, w2, misc_all = gather(in_weight, out_weight, misc)
    w1 = w1.reshape(H, C)
    w2 = w2.reshape(H, C)
    probe = misc_all[:, :TAPROWS, :CPART].transpose(1, 0, 2).reshape(TAPROWS, C)
    ibias = misc_all[:, TAPROWS:, :].reshape(N_MP, 8 * LANE)[:, :HPART].reshape(1, H)

    image = mp // 8
    top = 2 * lax.rem(mp, 8)
    side = lax.dynamic_slice_in_dim(shapes, image, 1, 0)[0]
    cells = jnp.arange(SIDE, dtype=jnp.int32)
    picture = lax.dynamic_slice_in_dim(canvas, image, 1, 0)[0]
    inside = ((cells[:, None] < side[0]) & (cells[None, :] < side[1])).astype(BF16)
    masked = jnp.pad(picture * inside[:, :, None], ((3, 3), (3, 5), (0, 0)))
    window = lax.dynamic_slice_in_dim(masked, top, KS + 1, 0)
    mine = lax.dynamic_slice_in_dim(picture, top, 2, 0)
    aim = lax.dynamic_slice(target, (image, top, 0, 0), (1, 2, SIDE, C))[0]
    diff = (aim.astype(F32) - mine.astype(F32)).astype(BF16).reshape(ROWS, C)
    mask = lax.dynamic_slice_in_dim(inside, top, 2, 0).astype(F32).reshape(ROWS, 1)
    mask = jnp.broadcast_to(mask, (ROWS, LANE))

    part, q1, *saved = first_stage(
        window,
        diff,
        mask,
        kernel,
        kernel_bias.reshape(1, C),
        norm_gain.reshape(1, C),
        norm_bias.reshape(1, C),
        ibias,
        out_bias.reshape(1, C),
        probe,
        w1,
        w2,
    )
    product = all_reduce(part, 0)
    part, q2, terms = second_stage(
        product, window, mask, norm_gain.reshape(1, C), q1, saved, w1, w2
    )
    product = all_reduce(part, 1)
    vector, scalars = last_stage(product, q1, q2, terms)
    krylov = lax.dynamic_slice(vector, (0, mp * CPART), (TAPS, CPART))
    return krylov, scalars[0, 3:4], scalars[0, 0:3]


def solution(mesh):
    placed = (
        P("dp", None, None, None),
        P("dp", None, None, None),
        P(),
        P(),
        P(),
        P(),
        P("mp", None),
        P("mp"),
        P("mp", None),
        P(),
        P(None, "mp"),
        P("dp", None),
        P("dp", None, None),
    )
    return jax.shard_map(
        per_device, mesh=mesh, in_specs=placed, out_specs=(P(None, "mp"), P(), P()), check_vma=False
    )
```

```python
import jax
import jax.numpy as jnp
from jax import lax
from jax.experimental import pallas as pl
from jax.experimental.pallas import tpu as pltpu
from jax.sharding import PartitionSpec as P

C = 1408
H = 5632
KS = 7
SIDE = 16
TAPS = 49
TOKENS = 2048
N_MP = 16
N_DP = 8
HPART = H // N_MP
HALF = HPART // 2
CPART = C // N_MP
ROWS = 32
LANE = 128
CBLK = C // LANE
HBLK = 1408
NHB = H // HBLK
TAPROWS = 56
TILES = 80
CHUNK = TILES // N_MP

EDGE = 64
MIDDLE = HALF - 2 * EDGE
PLANE = EDGE + MIDDLE
LAG_X = 4
LAG_FORWARD = 7

layer_eps = 1e-06
vector_eps = 1e-06
half_root = 0.7071067811865476
density_scale = 0.3989422804014327

MESH = pl.DeviceIdType.MESH
VMEM_BIG = 64 * 1024 * 1024 - 512 * 1024
F32 = jnp.float32
BF16 = jnp.bfloat16


def vmem():
    return pl.BlockSpec(memory_space=pltpu.VMEM)


def hbm():
    return pl.BlockSpec(memory_space=pl.ANY)


def rows_dot_t(left, right):
    return lax.dot_general(
        left, right, (((1,), (1,)), ((), ())), preferred_element_type=F32
    )


def rows_dot(left, right):
    return jnp.dot(left, right, preferred_element_type=F32)


def mean_rows(values):
    return jnp.sum(values, axis=1, keepdims=True) * (1.0 / C)


def total(values):
    return jnp.sum(jnp.sum(values, axis=1, keepdims=True), axis=0, keepdims=True)


def hidden(b):
    return pl.ds(pl.multiple_of(b * HBLK, HBLK), HBLK)


def convolve(xf_ref, taps_ref, out_ref, bias=None):
    def body(cb, carry):
        lanes = pl.ds(pl.multiple_of(cb * LANE, LANE), LANE)
        sums = [jnp.zeros((SIDE, LANE), F32) for _ in range(2)]
        for j in range(KS):
            for r in range(KS + 1):
                x = xf_ref[r, pl.ds(j, SIDE), lanes]
                for p in range(2):
                    i = r - p
                    if 0 <= i < KS:
                        sums[p] = sums[p] + x * taps_ref[pl.ds(i * KS + j, 1), lanes]
        for p in range(2):
            value = sums[p]
            if bias is not None:
                value = value + bias[pl.ds(0, 1), lanes]
            out_ref[pl.ds(p * SIDE, SIDE), lanes] = value
        return carry

    lax.fori_loop(0, CBLK, body, 0)


def correlate(xf_ref, grads_ref, out_ref):
    out_ref[...] = jnp.zeros_like(out_ref)

    def body(cb, carry):
        lanes = pl.ds(pl.multiple_of(cb * LANE, LANE), LANE)
        g = [[grads_ref[pl.ds(p * SIDE + 8 * h, 8), lanes] for h in range(2)] for p in range(2)]
        for j in range(KS):
            xs = [
                [xf_ref[r, pl.ds(j + 8 * h, 8), lanes] for h in range(2)] for r in range(KS + 1)
            ]
            for i in range(KS):
                acc = xs[i][0] * g[0][0] + xs[i][1] * g[0][1]
                acc = acc + xs[i + 1][0] * g[1][0] + xs[i + 1][1] * g[1][1]
                tap = i * KS + j
                out_ref[(tap // 8) * CBLK + cb, pl.ds(tap % 8, 1), :] = jnp.sum(
                    acc, axis=0, keepdims=True
                ) * (1.0 / TOKENS)
        return carry

    lax.fori_loop(0, CBLK, body, 0)


def untile(w_ref, flat_ref):
    for rb in range(TAPROWS // 8):
        for cb in range(CBLK):
            flat_ref[pl.ds(8 * rb, 8), pl.ds(LANE * cb, LANE)] = w_ref[rb * CBLK + cb]


def send(src, dst, ssem, rsem, **dev):
    copy = pltpu.make_async_remote_copy(
        src_ref=src, dst_ref=dst, send_sem=ssem, recv_sem=rsem, device_id=dev, device_id_type=MESH
    )
    copy.start()
    return copy


def all_reduce(p_ref, o_ref, in1, in2, sems):
    dp = lax.axis_index("dp")
    mp = lax.axis_index("mp")
    s1, r1, s2, r2, s3, r3 = sems
    first = []
    for r in range(1, N_MP):
        peer = lax.rem(mp + r, N_MP)
        first.append(
            send(p_ref.at[pl.ds(peer * CHUNK, CHUNK)], in1.at[r], s1.at[r], r1.at[r], mp=peer)
        )
    value = p_ref[pl.ds(mp * CHUNK, CHUNK)]
    for r in range(1, N_MP):
        first[r - 1].wait_recv()
        value = value + in1[r]
    in2[dp] = value
    second = []
    for r in range(1, N_DP):
        peer = lax.rem(dp + r, N_DP)
        second.append(send(in2.at[dp], in2.at[dp], s2.at[r], r2.at[r], dp=peer))
    for copy in second:
        copy.wait_recv()
    value = in2[0]
    for d in range(1, N_DP):
        value = value + in2[d]
    mine = pl.ds(mp * CHUNK, CHUNK)
    o_ref[mine] = value
    third = []
    for r in range(1, N_MP):
        peer = lax.rem(mp + r, N_MP)
        third.append(send(o_ref.at[mine], o_ref.at[mine], s3.at[r], r3.at[r], mp=peer))
    for copy in third:
        copy.wait_recv()
    return first + second + third


def lanczos_kernel(
    w1_ref,
    w2_ref,
    probe_ref,
    bias_ref,
    vec_ref,
    kernel_ref,
    shapes_ref,
    canvas_ref,
    target_ref,
    out_ref,
    scal_ref,
    w1s,
    w2s,
    probes,
    biases,
    xb_ref,
    tb_ref,
    xf_ref,
    tan_ref,
    acc_ref,
    slope_ref,
    curv_ref,
    tpre_ref,
    normed_ref,
    feat_ref,
    q_ref,
    q2_ref,
    part_ref,
    part2_ref,
    prod_ref,
    prod2_ref,
    in1a,
    in2a,
    in1b,
    in2b,
    psend,
    precv,
    xsend,
    xrecv,
    fsend,
    frecv,
    msend,
    mrecv,
    lsem,
    *arsems,
):
    dp = lax.axis_index("dp")
    mp = lax.axis_index("mp")
    core = lax.rem(dp, 2)
    x = dp // 2
    odd = lax.rem(x, 2)
    sib = dp + 1 - 2 * core
    z = mp // 4
    y = lax.rem(mp, 4)

    def at(dz, dy):
        return lax.rem(z + dz, 4) * 4 + lax.rem(y + dy, 4)

    barrier = pltpu.get_barrier_semaphore()
    for r in range(1, N_MP):
        pl.semaphore_signal(
            barrier, inc=1, device_id={"mp": lax.rem(mp + r, N_MP)}, device_id_type=MESH
        )
    for r in range(1, N_DP):
        pl.semaphore_signal(
            barrier, inc=1, device_id={"dp": lax.rem(dp + r, N_DP)}, device_id_type=MESH
        )

    image = mp // 8
    top = 2 * lax.rem(mp, 8)
    local = []

    def fetch(src, dst):
        copy = pltpu.make_async_copy(src, dst, lsem.at[len(local)])
        copy.start()
        local.append(copy)

    for r in range(KS + 1):
        row = lax.rem(top + r + SIDE - 3, SIDE)
        fetch(canvas_ref.at[image, row], xb_ref.at[r])
    for p in range(2):
        fetch(target_ref.at[image, top + p], tb_ref.at[p])
    fetch(w1_ref, w1s.at[pl.ds(0, HPART)])
    fetch(w2_ref, w2s.at[pl.ds(0, HPART)])
    fetch(probe_ref, probes.at[mp])
    fetch(bias_ref, biases.at[0])

    pl.semaphore_wait(barrier, N_MP + N_DP - 2)

    own = (w1_ref, w2_ref)
    ws = (w1s, w2s)
    started = []

    def offsets(colour, first, second):
        return (second, first) if colour == 0 else (first, second)

    def slot_of(dz, dy):
        return (dz % 4) * 4 + dy % 4

    def rows(slot, off, n):
        return pl.ds(pl.multiple_of(slot * HPART + core * HALF + off, 16), n)

    keys = [{}, {}]

    def go(colour, key, first, second, off, n, axis, sign):
        k = keys[colour].setdefault(key, len(keys[colour]))
        dz, dy = offsets(colour, first, second)
        move = 1 if sign == 0 else 3
        pz, py = offsets(colour, *((move, 0) if axis == 0 else (0, move)))
        src = own[colour] if (dz, dy) == (0, 0) else ws[colour]
        copy = send(
            src.at[rows(slot_of(dz, dy), off, n)],
            ws[colour].at[rows(slot_of(dz - pz, dy - py), off, n)],
            psend.at[colour, k],
            precv.at[colour, k],
            mp=at(pz, py),
        )
        started.append(copy)
        return copy

    plane_off = odd * EDGE
    copies = {}

    def relay_cut(flag):
        return PLANE // 2 // 16 * 16 + (16 if flag else 0) if PLANE // 2 % 16 else PLANE // 2

    def relay(colour, key, first, second, axis, sign, flag):
        cut = relay_cut(flag)
        off, n = (0, cut) if sign == 0 else (cut, PLANE - cut)
        copies[colour, key] = go(colour, key, first, second, plane_off + off, n, axis, sign)

    def spread(colour, first):
        for sign in range(2):
            key = ("s", first, sign)
            copies[colour, key] = go(colour, key, first, 0, plane_off, PLANE, 1, sign)

    xcopies = {}
    fcopies = {}

    def share(colour, first, second):
        dz, dy = offsets(colour, first, second)
        slot = slot_of(dz, dy)
        for sign in range(2):
            move = 1 if sign == 0 else 3
            piece = rows(slot, odd * PLANE + sign * (EDGE // 2), EDGE // 2)
            copy = send(
                ws[colour].at[piece],
                ws[colour].at[piece],
                xsend.at[colour, slot, sign],
                xrecv.at[colour, slot, sign],
                dp=lax.rem(x + move, 4) * 2 + core,
            )
            started.append(copy)
            xcopies[colour, slot, sign] = copy

    def forward(colour, slot, kind, off, n):
        piece = rows(slot, off, n)
        copy = send(
            ws[colour].at[piece],
            ws[colour].at[piece],
            fsend.at[colour, slot, kind],
            frecv.at[colour, slot, kind],
            dp=sib,
        )
        started.append(copy)
        fcopies[colour, slot, kind] = copy

    for colour in range(2):
        for sign in range(2):
            key = ("n", sign)
            copies[colour, key] = go(colour, key, 0, 0, plane_off, PLANE, 0, sign)
    for dz in range(4):
        for dy in range(4):
            if dz or dy:
                k = slot_of(dz, dy)
                copy = send(probe_ref, probes.at[mp], msend.at[0, k], mrecv.at[0, k], mp=at(dz, dy))
                started.append(copy)
                copies["probe", k] = copy
                k = slot_of(-dz, -dy)
                copy = send(
                    bias_ref, biases.at[k], msend.at[1, k], mrecv.at[1, k], mp=at(dz, dy)
                )
                started.append(copy)
                copies["bias", k] = copy
    for colour in range(2):
        spread(colour, 0)

    for copy in local:
        copy.wait()
    high = shapes_ref[image, 0]
    wide = shapes_ref[image, 1]
    column = lax.broadcasted_iota(jnp.int32, (SIDE, LANE), 0)
    in_row = jnp.where(column < wide, 1.0, 0.0)[:, 0:1]
    xf_ref[...] = jnp.zeros_like(xf_ref)
    for r in range(KS + 1):
        row = top + r - 3
        valid = jnp.where((row >= 0) & (row < high), 1.0, 0.0)
        xf_ref[r, pl.ds(3, SIDE), :] = xb_ref[r].astype(F32) * (in_row * valid)
    cell = lax.broadcasted_iota(jnp.int32, (ROWS, LANE), 0)
    lower = jnp.where(cell >= SIDE, 1, 0)
    mask = jnp.where((top + lower < high) & (cell - SIDE * lower < wide), 1.0, 0.0)[:, 0:1]
    gain = vec_ref[pl.ds(1, 1), :]

    convolve(xf_ref, kernel_ref, tan_ref, vec_ref)
    values = tan_ref[...].astype(BF16).astype(F32)
    centered = values - mean_rows(values)
    dev = jnp.sqrt(mean_rows(centered * centered) + layer_eps)
    normed = centered / dev
    normed_ref[...] = normed
    feat_ref[...] = (normed * gain + vec_ref[pl.ds(2, 1), :]).astype(BF16)
    acc_ref[...] = jnp.zeros_like(acc_ref)

    def run_block(slot):
        part = pl.ds(slot * HPART, HPART)
        pre = rows_dot_t(feat_ref[...], w1s[part, :]) + biases[slot][:, :HPART]
        phi = 0.5 * (1.0 + lax.erf(pre * half_root))
        density = density_scale * jnp.exp(-0.5 * pre * pre)
        slope_ref[:, part] = phi + pre * density
        curv_ref[:, part] = density * (2.0 - pre * pre)
        act = (pre * phi).astype(BF16)
        acc_ref[...] += rows_dot(act, w2s[part, :])

    events = []
    for sign in range(2):
        for colour in range(2):
            events.append((colour, 3 if sign == 0 else 1, 0, [("n", sign)]))
    for colour in range(2):
        events.append((colour, 2, 0, [("r", 0), ("r", 1)]))
    for first in (0, 3, 1, 2):
        for sign in range(2):
            for colour in range(2):
                events.append((colour, first, 3 if sign == 0 else 1, [("s", first, sign)]))
    for first in (0, 3, 1, 2):
        for colour in range(2):
            events.append((colour, first, 2, [("t", first, 0), ("t", first, 1)]))
    ready = {}
    queue = []

    def finish_x(index):
        colour, first, second, _ = events[index]
        slot = slot_of(*offsets(colour, first, second))
        for sign in range(2):
            xcopies[colour, slot, sign].wait_recv()
        forward(colour, slot, 1, (1 - odd) * PLANE, EDGE)
        ready[slot] = ready.get(slot, 0) + 1
        if ready[slot] == 2:
            queue.append((index, slot))

    def finish_block(slot):
        for colour in range(2):
            for kind in range(2):
                fcopies[colour, slot, kind].wait_recv()
        copies["bias", slot].wait_recv()
        run_block(slot)

    for index, (colour, first, second, waits) in enumerate(events):
        for key in waits:
            copies[colour, key].wait_recv()
        kind = waits[0][0]
        if kind == "n":
            sign = waits[0][1]
            relay(colour, ("r", sign), first, 0, 0, sign, colour)
        if kind in "nr":
            spread(colour, first)
        if kind == "s":
            sign = waits[0][2]
            relay(colour, ("t", first, sign), first, second, 1, sign, first % 2)
        share(colour, first, second)
        slot = slot_of(*offsets(colour, first, second))
        forward(colour, slot, 0, plane_off, PLANE)
        if index == 3:
            run_block(0)
        if index >= LAG_X:
            finish_x(index - LAG_X)
        while queue and queue[0][0] + LAG_FORWARD <= index:
            finish_block(queue.pop(0)[1])
        if index == 8:
            for k in range(1, N_MP):
                copies["probe", k].wait_recv()
            for i in range(N_MP):
                q_ref[:, pl.ds(i * CPART, CPART)] = probes[i][:, :CPART]
            probe = q_ref[...]
            q_ref[...] = probe / jnp.sqrt(total(probe * probe) + vector_eps)
            convolve(xf_ref, q_ref, tan_ref)
    for index in range(len(events) - LAG_X, len(events)):
        finish_x(index)
        if queue:
            finish_block(queue.pop(0)[1])
    while queue:
        finish_block(queue.pop(0)[1])

    diff = jnp.concatenate(
        [
            tb_ref[p].astype(F32) - xb_ref[3 + p].astype(F32)
            for p in range(2)
        ],
        axis=0,
    ).astype(BF16)
    residue = (acc_ref[...] + vec_ref[pl.ds(3, 1), :] - diff.astype(F32)).astype(BF16)
    acc_ref[...] = jnp.zeros_like(acc_ref)

    def backward(b, carry):
        hid = hidden(b)
        back = rows_dot_t(residue, w2s[hid, :])
        curv_ref[:, hid] = back * curv_ref[:, hid]
        back_pre = (back * slope_ref[:, hid]).astype(BF16)
        acc_ref[...] += rows_dot(back_pre, w1s[hid, :])
        return carry

    lax.fori_loop(0, NHB, backward, 0)
    grad_scaled = acc_ref[...] * gain
    normed = normed_ref[...]
    grad_corr = mean_rows(grad_scaled * normed)
    back_conv = (grad_scaled - mean_rows(grad_scaled) - normed * grad_corr) / dev

    def hessian(to_ref):
        t = tan_ref[...].astype(BF16).astype(F32)
        lift = mean_rows(normed * t)
        tan_hat = (t - mean_rows(t) - normed * lift) / dev
        rate = lift / dev
        feat = (tan_hat * gain).astype(BF16)
        acc_ref[...] = jnp.zeros_like(acc_ref)

        def up(b, carry):
            hid = hidden(b)
            tan_pre = rows_dot_t(feat, w1s[hid, :])
            tpre_ref[:, hid] = tan_pre
            act = (slope_ref[:, hid] * tan_pre).astype(BF16)
            acc_ref[...] += rows_dot(act, w2s[hid, :])
            return carry

        lax.fori_loop(0, NHB, up, 0)
        tan_out = acc_ref[...].astype(BF16)
        acc_ref[...] = jnp.zeros_like(acc_ref)

        def down(b, carry):
            hid = hidden(b)
            back = rows_dot_t(tan_out, w2s[hid, :])
            back_pre = (
                back * slope_ref[:, hid] + curv_ref[:, hid] * tpre_ref[:, hid]
            ).astype(BF16)
            acc_ref[...] += rows_dot(back_pre, w1s[hid, :])
            return carry

        lax.fori_loop(0, NHB, down, 0)
        scaled = acc_ref[...] * gain
        h1 = mean_rows(scaled)
        h2 = mean_rows(scaled * normed + grad_scaled * tan_hat)
        back = (scaled - h1 - tan_hat * grad_corr - normed * h2) / dev - back_conv * rate
        tan_ref[...] = back.astype(BF16).astype(F32) * mask
        correlate(xf_ref, tan_ref, to_ref)

    hessian(part_ref)
    reduced = all_reduce(part_ref, prod_ref, in1a, in2a, arsems[:6])
    untile(prod_ref, q2_ref)
    product = q2_ref[...]
    alpha_one = total(product * q_ref[...])
    remainder = product - alpha_one * q_ref[...]
    beta_one = jnp.sqrt(total(remainder * remainder) + vector_eps)
    q2_ref[...] = remainder / beta_one
    convolve(xf_ref, q2_ref, tan_ref)
    hessian(part2_ref)
    reduced = reduced + all_reduce(part2_ref, prod2_ref, in1b, in2b, arsems[6:])
    untile(prod2_ref, out_ref)
    product = out_ref[...]
    alpha_two = total(product * q2_ref[...])
    remainder = product - alpha_two * q2_ref[...] - beta_one * q_ref[...]
    beta_two = jnp.sqrt(total(remainder * remainder) + vector_eps)
    out_ref[...] = remainder / beta_two
    lane = lax.broadcasted_iota(jnp.int32, (8, LANE), 1)
    scal_ref[...] = jnp.where(
        lane == 0,
        alpha_two,
        jnp.where(lane == 1, beta_one, jnp.where(lane == 2, beta_two, alpha_one)),
    )
    for copy in started + reduced:
        copy.wait_send()


def lanczos(*args):
    dma = pltpu.SemaphoreType.DMA
    cells_c = pltpu.VMEM((ROWS, C), F32)
    cells_h = pltpu.VMEM((ROWS, H), F32)
    taps_c = pltpu.VMEM((TAPROWS, C), F32)
    tiles = pltpu.VMEM((TILES, 8, LANE), F32)
    from_mp = pltpu.VMEM((N_MP, CHUNK, 8, LANE), F32)
    from_dp = pltpu.VMEM((N_DP, CHUNK, 8, LANE), F32)
    return pl.pallas_call(
        lanczos_kernel,
        out_shape=(
            jax.ShapeDtypeStruct((TAPROWS, C), F32),
            jax.ShapeDtypeStruct((8, LANE), F32),
        ),
        in_specs=[vmem()] * 6 + [pl.BlockSpec(memory_space=pltpu.SMEM), hbm(), hbm()],
        out_specs=(vmem(), vmem()),
        scratch_shapes=[
            pltpu.VMEM((H, C), BF16),
            pltpu.VMEM((H, C), BF16),
            pltpu.VMEM((N_MP, TAPROWS, LANE), F32),
            pltpu.VMEM((N_MP, 1, 3 * LANE), F32),
            pltpu.VMEM((KS + 1, SIDE, C), BF16),
            pltpu.VMEM((2, SIDE, C), BF16),
            pltpu.VMEM((KS + 1, 24, C), F32),
            cells_c,
            cells_c,
            cells_h,
            cells_h,
            cells_h,
            cells_c,
            pltpu.VMEM((ROWS, C), BF16),
            taps_c,
            taps_c,
            tiles,
            tiles,
            tiles,
            tiles,
            from_mp,
            from_dp,
            from_mp,
            from_dp,
            dma((2, 20)),
            dma((2, 20)),
            dma((2, N_MP, 2)),
            dma((2, N_MP, 2)),
            dma((2, N_MP, 2)),
            dma((2, N_MP, 2)),
            dma((2, N_MP)),
            dma((2, N_MP)),
            dma((KS + 7,)),
        ]
        + 2 * [dma((N_MP,)), dma((N_MP,)), dma((N_DP,)), dma((N_DP,)), dma((N_MP,)), dma((N_MP,))],
        compiler_params=pltpu.CompilerParams(
            collective_id=0, has_side_effects=True, vmem_limit_bytes=VMEM_BIG
        ),
        name="lanczos",
    )(*args)


def per_device(
    canvas,
    target,
    kernel,
    kernel_bias,
    norm_gain,
    norm_bias,
    in_weight,
    in_bias,
    out_weight,
    out_bias,
    probe_vector,
    shapes,
    send_slots,
):
    mp = lax.axis_index("mp")
    vector, scalars = lanczos(
        in_weight,
        out_weight,
        jnp.pad(probe_vector, ((0, TAPROWS - TAPS), (0, LANE - CPART))),
        jnp.pad(in_bias, (0, 3 * LANE - HPART)).reshape(1, 3 * LANE),
        jnp.stack([kernel_bias, norm_gain, norm_bias, out_bias]),
        kernel,
        shapes,
        canvas,
        target,
    )
    krylov = lax.dynamic_slice(vector, (0, mp * CPART), (TAPS, CPART))
    return krylov, scalars[0, 3:4], scalars[0, 0:3]


def solution(mesh):
    placed = (
        P("dp", None, None, None),
        P("dp", None, None, None),
        P(),
        P(),
        P(),
        P(),
        P("mp", None),
        P("mp"),
        P("mp", None),
        P(),
        P(None, "mp"),
        P("dp", None),
        P("dp", None, None),
    )
    return jax.shard_map(
        per_device, mesh=mesh, in_specs=placed, out_specs=(P(None, "mp"), P(), P()), check_vma=False
    )
```
